32 devices in a mesh: dp: 16 (over z, y, x), tensor: 2 (over core).
Axes of the slice: x: 2, y: 2, z: 4, core: 2. Of those that a mesh axis runs over, the one named last changes fastest.
Arguments:
- hidden: bfloat16 [128, 4096], P('dp'), may hold values from -20 to 20
- gain: bfloat16 [4096], replicated, may hold values from 0.5 to 1.5
- head: bfloat16 [4096, 4096], P(('dp', 'tensor')), may hold values from -32 to 32
- moment: bfloat16 [4096, 4096], P(('dp', 'tensor')), may hold values from -6 to 6
- second: float32 [4096], P(('dp', 'tensor')), may hold values from 0.5 to 50
- labels: int32 [128], P('dp'), may hold values from 0 to 4095
Outputs:
- grad_hidden: bfloat16 [128, 4096], P('dp')
- grad_gain: float32 [4096], replicated
- head_new: bfloat16 [4096, 4096], P(('dp', 'tensor'))
- moment_new: bfloat16 [4096, 4096], P(('dp', 'tensor'))
- second_new: float32 [4096], P(('dp', 'tensor'))
The draws below stay inside these ranges and needn't reach their ends.
All inputs are finite; a program needn't handle non-finite values.
Results may differ from the reference program's by a relative error of at most 0.01.
Values may be sent and summed in bfloat16 or wider, within the bound.
A program may use at most 64 MiB of HBM per device.

```python
import math
import jax
import jax.numpy as jnp
from jax import lax

D = 4096
ROWS_OWN = 128
VOCAB = 4096
TOKENS = 128
N_DP = 16
N_TENSOR = 2


def pair_vectors(key):
    return jax.random.normal(jax.random.fold_in(key, 7), (4, D), jnp.float32)


def draw_hidden(key, part):
    own_key = jax.random.fold_in(key, 11)
    values = jnp.clip(jax.random.normal(own_key, (TOKENS, D), jnp.float32), -6.0, 6.0)
    aligned = jnp.clip(pair_vectors(key), -5.0, 5.0)
    values = jnp.concatenate([aligned, values[4:]], 0)
    return values.astype(jnp.bfloat16)


def draw_head(key, part):
    own_key = jax.random.fold_in(key, 13)
    sigma = 3.0 / math.sqrt(D)
    values = jnp.clip(sigma * jax.random.normal(own_key, (VOCAB, D), jnp.float32), -6.0 * sigma, 6.0 * sigma)
    aligned = jnp.clip(pair_vectors(key), -5.0, 5.0)
    strength = jnp.array([2.0, 3.0, 4.0, 5.0], jnp.float32)
    upper = aligned * (64.0 * strength[:, None]) / D + 0.3 * sigma * jax.random.normal(jax.random.fold_in(own_key, 3), (4, D), jnp.float32)
    lower = aligned * (64.0 * strength[:, None] - 2.0) / D + 0.3 * sigma * jax.random.normal(jax.random.fold_in(own_key, 4), (4, D), jnp.float32)
    paired = jnp.stack([upper, lower], 1).reshape(8, D)
    values = jnp.concatenate([paired, values[8:]], 0)
    return jnp.clip(values, -32.0, 32.0).astype(jnp.bfloat16)


def with_ends(entries, stream_key, least, largest):
    extent = entries.shape
    place = [jax.random.randint(jax.random.fold_in(stream_key, axis), (), 0, extent[axis]) for axis in range(len(extent))]
    entries = entries.at[tuple(place)].set(least)
    longest = extent.index(max(extent))
    place[longest] = (place[longest] + 1) % extent[longest]
    return entries.at[tuple(place)].set(largest)


def block_scale(key, dims, split, least, high):
    def one(axis_at, shards_of):
        steps = jax.random.uniform(jax.random.fold_in(jax.random.fold_in(key, 6), axis_at), (shards_of,), jnp.float32, least / len(split), high / len(split))
        return jnp.repeat(jnp.exp(steps), dims[axis_at] // shards_of).reshape((-1,) + (1,) * (len(dims) - axis_at - 1))

    level = one(*split[0])
    for cut in split[1:]:
        level = level * one(*cut)
    return level


def bell_draw(key, dims, scale, limit, shards=(), held_as=jnp.bfloat16):
    entries = jax.random.normal(key, dims, jnp.float32) * scale
    if len(shards) > 0:
        entries = block_scale(key, dims, shards, -0.22, 0.18) * entries
    return jnp.clip(entries, min=-limit, max=limit).astype(held_as)


def setup_inputs(seed: int = 0) -> dict:
    key_list = jax.random.split(jax.random.key(seed), 7)
    hidden = draw_hidden(jax.random.fold_in(key_list[6], 71), 0)
    gain = jnp.clip(1.0 + 0.1 * jax.random.normal(key_list[1], (D,), jnp.float32), 0.5, 1.5).astype(jnp.bfloat16)
    head = draw_head(jax.random.fold_in(key_list[6], 71), 0)
    moment = bell_draw(key_list[3], (VOCAB, D), 1.0, 6.0, ((0, 32),))
    second = jnp.clip(jnp.exp(math.log(50.0) - 4.6051702 * jax.random.uniform(key_list[4], (VOCAB,), jnp.float32) ** block_scale(key_list[4], (VOCAB,), ((0, 32),), -0.2, 0.2)), 0.5, 50.0)
    labels = with_ends(jax.random.randint(key_list[5], (TOKENS,), 0, VOCAB), jax.random.fold_in(key_list[5], 1), 0, VOCAB - 1).astype(jnp.int32)
    return {"hidden": hidden, "gain": gain, "head": head, "moment": moment, "second": second, "labels": labels}


loss_scale = 16.0
beta_one = 0.9
beta_two = 0.999
adam_eps = 1e-08
step_size = 0.02
norm_eps = 1e-05
bias_one = 1.0 - 0.9 ** 10
bias_two = 1.0 - 0.999 ** 10

def reference(hidden, gain, head, moment, second, labels):
    hidden_f = hidden.astype(jnp.float32)
    gain_f = gain.astype(jnp.float32)
    squares = lax.optimization_barrier(jnp.sum(hidden_f * hidden_f, axis=1))
    rstd = lax.rsqrt(squares / D + norm_eps)
    normed = (hidden_f * rstd[:, None] * gain_f).astype(jnp.bfloat16)
    block_rows = ROWS_OWN * N_TENSOR
    blocks = head.reshape(N_DP, block_rows, D)
    block_ids = jnp.arange(VOCAB, dtype=jnp.int32).reshape(N_DP, block_rows)

    def stats_step(running, window):
        run_max, run_sum = running
        logits = jnp.dot(normed, window.T, preferred_element_type=jnp.float32)
        new_max = jnp.maximum(run_max, lax.optimization_barrier(jnp.max(logits, axis=1)))
        new_sum = run_sum * jnp.exp(run_max - new_max) + lax.optimization_barrier(jnp.sum(jnp.exp(logits - new_max[:, None]), axis=1))
        return ((new_max, new_sum), None)
    start_max = jnp.full((TOKENS,), -1e+30, jnp.float32)
    start_sum = jnp.zeros((TOKENS,), jnp.float32)
    (row_max, row_sum), _ = lax.scan(stats_step, (start_max, start_sum), blocks)

    def grad_step(grad_acc, inputs):
        window, vocab_ids = inputs
        logits = jnp.dot(normed, window.T, preferred_element_type=jnp.float32)
        onehot = (labels[:, None] == vocab_ids[None, :]).astype(jnp.float32)
        probability = jnp.exp(logits - row_max[:, None]) / row_sum[:, None]
        dlogits = (loss_scale * (probability - onehot)).astype(jnp.bfloat16)
        grad_window = jnp.dot(dlogits.T, normed, preferred_element_type=jnp.float32)
        split_logits = dlogits.reshape(TOKENS, N_TENSOR, ROWS_OWN).astype(jnp.float32)
        split_rows = window.reshape(N_TENSOR, ROWS_OWN, D).astype(jnp.float32)
        partials = jnp.einsum('tkr,krd->ktd', split_logits, split_rows).astype(jnp.bfloat16)
        grad_acc = grad_acc + lax.optimization_barrier(jnp.sum(partials.astype(jnp.float32), axis=0))
        return (grad_acc, grad_window)
    grad_start = jnp.zeros((TOKENS, D), jnp.float32)
    grad_normed, grad_windows = lax.scan(grad_step, grad_start, (blocks, block_ids))
    grad_head = grad_windows.reshape(VOCAB, D)
    grad_gain = lax.optimization_barrier(jnp.sum(grad_normed * hidden_f * rstd[:, None], axis=0))
    inner_sums = lax.optimization_barrier(jnp.sum(grad_normed * gain_f * hidden_f, axis=1))
    grad_hidden = (rstd[:, None] * gain_f * grad_normed - hidden_f * (rstd ** 3)[:, None] * inner_sums[:, None] / D).astype(jnp.bfloat16)
    second_new = beta_two * second + (1.0 - beta_two) * lax.optimization_barrier(jnp.sum(grad_head * grad_head, axis=1)) / D
    first = beta_one * moment.astype(jnp.float32) + (1.0 - beta_one) * grad_head
    adam_step = first / bias_one / (jnp.sqrt(second_new / bias_two)[:, None] + adam_eps)
    head_new = (head.astype(jnp.float32) - step_size * adam_step).astype(jnp.bfloat16)
    return (grad_hidden, grad_gain, head_new, first.astype(jnp.bfloat16), second_new)
```

```python
import functools

import jax
import jax.numpy as jnp
from jax import lax
from jax.experimental import pallas as pl
from jax.experimental.pallas import tpu as pltpu
from jax.sharding import PartitionSpec as P

MESH = pl.DeviceIdType.MESH
LANES = 128
PLANE = 4
CHUNK = 512

D = 4096


loss_scale = 16.0
beta_one = 0.9
beta_two = 0.999
adam_eps = 1e-08
step_size = 0.02
norm_eps = 1e-05
bias_one = 1.0 - 0.9**10
bias_two = 1.0 - 0.999**10


def inverse_norm(values_f):
    squares = jnp.sum(values_f * values_f, axis=1)
    return lax.rsqrt(squares / D + norm_eps)


def softmax_grad(logits, targets, vocab_ids):
    local_max = jnp.max(logits, axis=1)
    local_sum = jnp.sum(jnp.exp(logits - local_max[:, None]), axis=1)
    global_max = lax.pmax(local_max, ("dp", "tensor"))
    global_sum = lax.psum(local_sum * jnp.exp(local_max - global_max), ("dp", "tensor"))
    onehot = (targets[:, None] == vocab_ids[None, :]).astype(jnp.float32)
    probability = jnp.exp(logits - global_max[:, None]) / global_sum[:, None]
    return (loss_scale * (probability - onehot)).astype(jnp.bfloat16)


def norm_backward(grad_normed, hidden_part, rstd_part, gain_f):
    inner_sums = jnp.sum(grad_normed * gain_f * hidden_part, axis=1)
    return (
        rstd_part[:, None] * gain_f * grad_normed
        - hidden_part * (rstd_part**3)[:, None] * inner_sums[:, None] / D
    ).astype(jnp.bfloat16)


def local(hidden, gain, head, moment, second, labels):
    hidden_f = hidden.astype(jnp.float32)
    gain_f = gain.astype(jnp.float32)
    rstd = inverse_norm(hidden_f)
    normed = (hidden_f * rstd[:, None] * gain_f).astype(jnp.bfloat16)
    normed_all = lax.all_gather(normed, "dp", axis=0, tiled=True)
    all_labels = lax.all_gather(labels, "dp", axis=0, tiled=True)
    own_rows = head.shape[0]
    tensor_count = lax.axis_size("tensor")
    dp_count = lax.axis_size("dp")
    owner = lax.axis_index("dp") * tensor_count + lax.axis_index("tensor")
    vocab_ids = owner * own_rows + jnp.arange(own_rows, dtype=jnp.int32)
    logits = lax.dot_general(
        normed_all, head, (((1,), (1,)), ((), ())), preferred_element_type=jnp.float32
    )
    dlogits = softmax_grad(logits, all_labels, vocab_ids)
    grad_head = lax.dot_general(
        dlogits, normed_all, (((0,), (0,)), ((), ())), preferred_element_type=jnp.float32
    )
    share_rows = hidden.shape[0] // tensor_count
    ordered = dlogits.reshape(dp_count, tensor_count, share_rows, own_rows).transpose(1, 0, 2, 3)
    ordered = ordered.reshape(tensor_count * dp_count * share_rows, own_rows)
    tensor_sum = lax.psum_scatter(
        jnp.dot(ordered, head, preferred_element_type=jnp.float32).astype(jnp.bfloat16),
        "tensor",
        scatter_dimension=0,
        tiled=True,
    ).astype(jnp.float32)
    full_sum = lax.psum(tensor_sum, "dp")
    grad_normed = lax.dynamic_slice_in_dim(
        full_sum, lax.axis_index("dp") * share_rows, share_rows, 0
    )
    offset = lax.axis_index("tensor") * share_rows
    hidden_part = lax.dynamic_slice_in_dim(hidden_f, offset, share_rows, 0)
    rstd_part = lax.dynamic_slice_in_dim(rstd, offset, share_rows, 0)
    grad_gain = lax.psum(
        jnp.sum(grad_normed * hidden_part * rstd_part[:, None], axis=0), ("dp", "tensor")
    )
    part_grad = norm_backward(grad_normed, hidden_part, rstd_part, gain_f)
    grad_hidden = lax.all_gather(part_grad, "tensor", axis=0, tiled=True)
    row_sums = jnp.sum(grad_head * grad_head, axis=1)
    second_new = beta_two * second + (1.0 - beta_two) * row_sums / D
    first = beta_one * moment.astype(jnp.float32) + (1.0 - beta_one) * grad_head
    adam_step = first / bias_one / (jnp.sqrt(second_new / bias_two)[:, None] + adam_eps)
    head_new = (head.astype(jnp.float32) - step_size * adam_step).astype(jnp.bfloat16)
    return (grad_hidden, grad_gain, head_new, first.astype(jnp.bfloat16), second_new)


def wide(values):
    return values.astype(jnp.float32)


def narrow(values):
    return values.astype(jnp.bfloat16)


def fused_kernel(
    layers,
    hidden_ref,
    gain_ref,
    head_hbm,
    moment_hbm,
    second_ref,
    labels_ref,
    grad_hidden_ref,
    grad_gain_ref,
    head_out,
    moment_out,
    second_out,
    gathered,
    normed,
    head,
    moment,
    gain_wide,
    grad_head,
    head_new,
    moment_new,
    stat_own,
    stats,
    pair_out,
    pair_in,
    plane_out,
    plane_in,
    plane_sum,
    line_out,
    line_in,
    message,
    columns_in,
    gather_recv,
    gather_line,
    gather_plane,
    gather_pair,
    stat_send,
    stat_recv,
    pair_sems,
    plane_sems,
    line_sems,
    message_send,
    message_recv,
    local_sems,
):
    groups = layers * PLANE
    devices = groups * 2
    tokens, width = normed.shape
    own_tokens = hidden_ref.shape[0]
    own_rows = head.shape[0]
    half = width // 2
    dp = lax.axis_index("dp")
    core = lax.axis_index("tensor")
    other = 1 - core
    layer = lax.div(dp, PLANE)
    spot = lax.rem(dp, PLANE)
    me = dp * 2 + core
    own_block = (core * PLANE + spot) * layers + layer

    def at(index):
        return (lax.div(index, 2), lax.rem(index, 2))

    def partner(step):
        return lax.rem(me + step, devices)

    def block_of(index):
        target_dp, target_core = at(index)
        return (target_core * PLANE + lax.rem(target_dp, PLANE)) * layers + lax.div(
            target_dp, PLANE
        )

    def remote(source, target, send_sem, recv_sem, device):
        return pltpu.make_async_remote_copy(
            src_ref=source,
            dst_ref=target,
            send_sem=send_sem,
            recv_sem=recv_sem,
            device_id=device,
            device_id_type=MESH,
        )

    head_copy = pltpu.make_async_copy(head_hbm, head, local_sems.at[0])
    head_copy.start()
    moment_copy = pltpu.make_async_copy(moment_hbm, moment, local_sems.at[1])
    moment_copy.start()

    barrier = pltpu.get_barrier_semaphore()

    def greet(step, carry):
        pl.semaphore_signal(barrier, inc=1, device_id=at(partner(step)), device_id_type=MESH)
        return carry

    lax.fori_loop(1, devices, greet, 0)

    gain_wide[...] = wide(gain_ref[...])
    hidden_f = wide(hidden_ref[...])
    rstd = lax.rsqrt(jnp.sum(hidden_f * hidden_f, axis=1, keepdims=True) / width + norm_eps)
    own = narrow(hidden_f * rstd * gain_wide[...])
    gathered[0, dp] = own[:, :half]
    gathered[1, dp] = own[:, half:]
    pl.semaphore_wait(barrier, devices - 1)

    def shard(side, group, send_sem, device):
        block = gathered.at[side, group]
        return remote(block, block, send_sem, gather_recv.at[side, group], device)

    def across(step):
        return lax.rem(layer + step, layers)

    def beside(step):
        return lax.rem(spot + step, PLANE)

    def line_copy(step):
        return shard(core, dp, gather_line.at[step], (across(step) * PLANE + spot, core))

    def plane_copy(row, step):
        return shard(
            core,
            across(row) * PLANE + spot,
            gather_plane.at[row, step],
            (layer * PLANE + beside(step), core),
        )

    def pair_copy(side, row, step):
        group = across(row) * PLANE + beside(step)
        return shard(side, group, gather_pair.at[row, step], (dp, other))

    for step in range(1, layers):
        line_copy(step).start()
    for step in range(1, PLANE):
        plane_copy(0, step).start()
    for row in range(1, layers):
        pair_copy(core, row, 0).wait_recv()
        for step in range(1, PLANE):
            plane_copy(row, step).start()
        pair_copy(core, row, 0).start()
    for row in range(layers):
        for step in range(1, PLANE):
            pair_copy(core, row, step).wait_recv()
            pair_copy(core, row, step).start()

    def half_logits(side):
        span = pl.ds(pl.multiple_of(side * half, half), half)
        normed[:, span] = narrow(wide(gathered[side]).reshape(tokens, half))
        return lax.dot_general(
            head[:, span],
            normed[:, span],
            (((1,), (1,)), ((), ())),
            preferred_element_type=jnp.float32,
        )

    head_copy.wait()
    logits = half_logits(core)
    for row in range(layers):
        for step in range(PLANE):
            if row + step > 0:
                pair_copy(other, row, step).wait_recv()
    logits = logits + half_logits(other)

    lane = lax.broadcasted_iota(jnp.int32, (1, tokens), 1)
    targets = jnp.zeros((1, tokens), jnp.int32)
    for item in range(own_tokens):
        targets = jnp.where(lane == dp * own_tokens + item, labels_ref[item], targets)
    targets = jnp.where(core == 0, targets, 0)
    local_max = jnp.max(logits, axis=0, keepdims=True)
    local_sum = jnp.sum(jnp.exp(logits - local_max), axis=0, keepdims=True)
    place = lax.broadcasted_iota(jnp.int32, stat_own.shape, 0)
    packet = jnp.where(place == 0, local_max, jnp.where(place == 1, local_sum, wide(targets)))
    stat_own[...] = packet
    stats[me] = packet

    def stat_copy(step):
        target = partner(step)
        return remote(
            stat_own, stats.at[me], stat_send.at[step], stat_recv.at[me], at(target)
        )

    def stat_start(step, carry):
        stat_copy(step).start()
        return carry

    def stat_wait(step, carry):
        source = partner(step)
        remote(
            stat_own, stats.at[source], stat_send.at[step], stat_recv.at[source], at(source)
        ).wait_recv()
        return carry

    lax.fori_loop(1, devices, stat_start, 0)
    lax.fori_loop(1, devices, stat_wait, 0)

    every = stats[...]
    every_max = every[:, 0:1, :]
    global_max = jnp.max(every_max, axis=0)
    global_sum = jnp.sum(every[:, 1:2, :] * jnp.exp(every_max - global_max), axis=0)
    all_targets = jnp.sum(every[:, 2:3, :], axis=0).astype(jnp.int32)
    vocab = me * own_rows + lax.broadcasted_iota(jnp.int32, (own_rows, tokens), 0)
    onehot = wide(vocab == all_targets)
    probability = jnp.exp(logits - global_max) / global_sum
    scaled = loss_scale * (probability - onehot)
    by_row = narrow(scaled)
    by_token = narrow(scaled.T)

    quarter = half // PLANE

    def partial(side, step):
        start = side * half + beside(step) * quarter
        return jnp.dot(
            by_token,
            head[:, pl.ds(pl.multiple_of(start, quarter), quarter)],
            preferred_element_type=jnp.float32,
        )

    order = [*range(1, PLANE), 0]

    def pair_move(step):
        return remote(
            pair_out.at[step],
            pair_in.at[step],
            pair_sems.at[0, step],
            pair_sems.at[1, step],
            (dp, other),
        )

    def plane_move(step):
        return remote(
            plane_out.at[step],
            plane_in.at[step],
            plane_sems.at[0, step],
            plane_sems.at[1, step],
            (layer * PLANE + beside(step), core),
        )

    def line_move(step):
        return remote(
            line_out.at[step],
            line_in.at[step],
            line_sems.at[0, step],
            line_sems.at[1, step],
            (across(step) * PLANE + spot, core),
        )

    for step in order:
        pair_out[step] = narrow(partial(other, step))
        pair_move(step).start()
    for step in order:
        mine = partial(core, step)
        pair_move(step).wait_recv()
        mine = mine + wide(pair_in[step])
        if step > 0:
            plane_out[step] = narrow(mine)
            plane_move(step).start()
        else:
            plane_sum[...] = mine

    squares = jnp.zeros((own_rows, 1), jnp.float32)
    for start in range(0, width, CHUNK):
        piece = jnp.dot(
            by_row, normed[:, start : start + CHUNK], preferred_element_type=jnp.float32
        )
        grad_head[:, start : start + CHUNK] = piece
        squares = squares + jnp.sum(piece * piece, axis=1, keepdims=True)
    second_wide = jnp.broadcast_to(second_ref[...], (LANES, own_rows)).T
    second_new = beta_two * second_wide + (1.0 - beta_two) * squares / width
    second_out[...] = second_new.T[0:1, :]
    scale = (step_size / bias_one) / (jnp.sqrt(second_new / bias_two) + adam_eps)
    scale = scale[:, 0:1]
    moment_copy.wait()

    def adam(index, carry):
        span = pl.ds(pl.multiple_of(index * CHUNK, CHUNK), CHUNK)
        first = beta_one * wide(moment[:, span]) + (1.0 - beta_one) * grad_head[:, span]
        moment_new[:, span] = narrow(first)
        head_new[:, span] = narrow(wide(head[:, span]) - first * scale)
        return carry

    lax.fori_loop(0, width // CHUNK, adam, 0)
    head_store = pltpu.make_async_copy(head_new, head_out, local_sems.at[2])
    head_store.start()
    moment_store = pltpu.make_async_copy(moment_new, moment_out, local_sems.at[3])
    moment_store.start()

    total = plane_sum[...]
    for step in range(1, PLANE):
        plane_move(step).wait_recv()
        total = total + wide(plane_in[step])
    plane_sum[...] = total

    def line_span(step):
        return pl.ds(pl.multiple_of(across(step) * LANES, LANES), LANES)

    for step in range(1, layers):
        line_out[step] = narrow(plane_sum[:, line_span(step)])
        line_move(step).start()
    grad_normed = plane_sum[:, line_span(0)]
    for step in range(1, layers):
        line_move(step).wait_recv()
        grad_normed = grad_normed + wide(line_in[step])

    own_span = pl.ds(pl.multiple_of(own_block * LANES, LANES), LANES)
    gain_part = (
        jnp.sum(grad_normed * wide(normed[:, own_span]), axis=0, keepdims=True)
        / gain_wide[:, own_span]
    )
    gain_high = wide(narrow(gain_part))
    gain_low = gain_part - gain_high
    row = lax.broadcasted_iota(jnp.int32, (own_tokens, LANES), 0)
    tail = jnp.where(row == 0, gain_high, jnp.where(row == 1, gain_low, 0.0))
    sums = grad_normed.reshape(groups, own_tokens, LANES)
    tails = jnp.broadcast_to(tail[None], sums.shape)
    message[...] = narrow(jnp.concatenate([sums, tails], axis=1))
    columns_in[own_block] = message[dp]

    def message_start(step, carry):
        target = at(partner(step))
        remote(
            message.at[target[0]],
            columns_in.at[own_block],
            message_send.at[step],
            message_recv.at[own_block],
            target,
        ).start()
        return carry

    def message_wait(step, carry):
        source = partner(step)
        block = block_of(source)
        remote(
            message.at[0],
            columns_in.at[block],
            message_send.at[step],
            message_recv.at[block],
            at(source),
        ).wait_recv()
        return carry

    lax.fori_loop(1, devices, message_start, 0)

    for step in range(1, layers):
        line_copy(step).wait_send()
        line_move(step).wait_send()
    for step_row in range(layers):
        for step in range(PLANE):
            if step > 0:
                plane_copy(step_row, step).wait_send()
            if step_row + step > 0:
                pair_copy(core, step_row, step).wait_send()
    for step in range(PLANE):
        pair_move(step).wait_send()
        if step > 0:
            plane_move(step).wait_send()

    def stat_done(step, carry):
        stat_copy(step).wait_send()
        return carry

    lax.fori_loop(1, devices, stat_done, 0)
    lax.fori_loop(1, devices, message_wait, 0)

    pieces = []
    for block in range(devices):
        arrived = wide(columns_in[block])
        pieces.append(arrived[:own_tokens])
        grad_gain_ref[block : block + 1, :] = (
            arrived[own_tokens : own_tokens + 1] + arrived[own_tokens + 1 : own_tokens + 2]
        )
    summed = jnp.concatenate(pieces, axis=1) * gain_wide[...]
    inner = jnp.sum(summed * hidden_f, axis=1, keepdims=True)
    grad_hidden_ref[...] = narrow(
        rstd * summed - hidden_f * (rstd * rstd * rstd * inner / width)
    )

    def message_done(step, carry):
        target = at(partner(step))
        remote(
            message.at[target[0]],
            columns_in.at[own_block],
            message_send.at[step],
            message_recv.at[own_block],
            target,
        ).wait_send()
        return carry

    lax.fori_loop(1, devices, message_done, 0)
    head_store.wait()
    moment_store.wait()


def fused(groups, hidden, gain, head, moment, second, labels):
    own_tokens, width = hidden.shape
    own_rows = head.shape[0]
    layers = groups // PLANE
    tokens = groups * own_tokens
    devices = groups * 2
    bf16, f32 = jnp.bfloat16, jnp.float32
    quarter = width // 2 // PLANE
    vmem = pl.BlockSpec(memory_space=pltpu.VMEM)
    anywhere = pl.BlockSpec(memory_space=pl.ANY)
    dma = pltpu.SemaphoreType.DMA
    grad_hidden, grad_gain, head_new, moment_new, second_new = pl.pallas_call(
        functools.partial(fused_kernel, layers),
        out_shape=(
            jax.ShapeDtypeStruct(hidden.shape, bf16),
            jax.ShapeDtypeStruct((devices, LANES), f32),
            jax.ShapeDtypeStruct(head.shape, bf16),
            jax.ShapeDtypeStruct(head.shape, bf16),
            jax.ShapeDtypeStruct((1, own_rows), f32),
        ),
        in_specs=[
            vmem,
            vmem,
            anywhere,
            anywhere,
            vmem,
            pl.BlockSpec(memory_space=pltpu.SMEM),
        ],
        out_specs=(vmem, vmem, anywhere, anywhere, vmem),
        scratch_shapes=[
            pltpu.VMEM((2, groups, own_tokens, width // 2), bf16),
            pltpu.VMEM((tokens, width), bf16),
            pltpu.VMEM((own_rows, width), bf16),
            pltpu.VMEM((own_rows, width), bf16),
            pltpu.VMEM((1, width), f32),
            pltpu.VMEM((own_rows, width), f32),
            pltpu.VMEM((own_rows, width), bf16),
            pltpu.VMEM((own_rows, width), bf16),
            pltpu.VMEM((8, tokens), f32),
            pltpu.VMEM((devices, 8, tokens), f32),
            pltpu.VMEM((PLANE, tokens, quarter), bf16),
            pltpu.VMEM((PLANE, tokens, quarter), bf16),
            pltpu.VMEM((PLANE, tokens, quarter), bf16),
            pltpu.VMEM((PLANE, tokens, quarter), bf16),
            pltpu.VMEM((tokens, quarter), f32),
            pltpu.VMEM((layers, tokens, LANES), bf16),
            pltpu.VMEM((layers, tokens, LANES), bf16),
            pltpu.VMEM((groups, 2 * own_tokens, LANES), bf16),
            pltpu.VMEM((devices, 2 * own_tokens, LANES), bf16),
            dma((2, groups)),
            dma((layers,)),
            dma((layers, PLANE)),
            dma((layers, PLANE)),
            dma((devices,)),
            dma((devices,)),
            dma((2, PLANE)),
            dma((2, PLANE)),
            dma((2, layers)),
            dma((devices,)),
            dma((devices,)),
            dma((4,)),
        ],
        compiler_params=pltpu.CompilerParams(
            collective_id=0, has_side_effects=True, vmem_limit_bytes=40 * 1024 * 1024
        ),
    )(hidden, gain.reshape(1, width), head, moment, second.reshape(1, own_rows), labels)
    return (
        grad_hidden,
        grad_gain.reshape(width),
        head_new,
        moment_new,
        second_new.reshape(own_rows),
    )


def fits(mesh, hidden, head):
    groups, cores = mesh.shape["dp"], mesh.shape["tensor"]
    return (
        cores == 2
        and groups % PLANE == 0
        and hidden.shape == (LANES, groups * cores * LANES)
        and hidden.shape[0] == groups * 8
        and head.shape[0] == groups * cores * LANES
    )


def solution(mesh):
    placed = (
        P("dp", None),
        P(),
        P(("dp", "tensor"), None),
        P(("dp", "tensor"), None),
        P(("dp", "tensor")),
        P("dp"),
    )

    def whole(hidden, gain, head, moment, second, labels):
        body = local
        if fits(mesh, hidden, head):
            body = functools.partial(fused, mesh.shape["dp"])
        return jax.shard_map(
            body,
            mesh=mesh,
            in_specs=placed,
            out_specs=(
                P("dp", None),
                P(),
                P(("dp", "tensor"), None),
                P(("dp", "tensor"), None),
                P(("dp", "tensor")),
            ),
            check_vma=False,
        )(hidden, gain, head, moment, second, labels)

    return whole
```

```python
import functools

import jax
import jax.numpy as jnp
from jax import lax
from jax.experimental import pallas as pl
from jax.experimental.pallas import tpu as pltpu
from jax.sharding import PartitionSpec as P

MESH = pl.DeviceIdType.MESH
LANES = 128
PLANE = 4
CHUNK = 512
VMEM_BYTES = 61440 * 1024

D = 4096


loss_scale = 16.0
beta_one = 0.9
beta_two = 0.999
adam_eps = 1e-08
step_size = 0.02
norm_eps = 1e-05
bias_one = 1.0 - 0.9**10
bias_two = 1.0 - 0.999**10


def inverse_norm(values_f):
    squares = jnp.sum(values_f * values_f, axis=1)
    return lax.rsqrt(squares / D + norm_eps)


def softmax_grad(logits, targets, vocab_ids):
    local_max = jnp.max(logits, axis=1)
    local_sum = jnp.sum(jnp.exp(logits - local_max[:, None]), axis=1)
    global_max = lax.pmax(local_max, ("dp", "tensor"))
    global_sum = lax.psum(local_sum * jnp.exp(local_max - global_max), ("dp", "tensor"))
    onehot = (targets[:, None] == vocab_ids[None, :]).astype(jnp.float32)
    probability = jnp.exp(logits - global_max[:, None]) / global_sum[:, None]
    return (loss_scale * (probability - onehot)).astype(jnp.bfloat16)


def norm_backward(grad_normed, hidden_part, rstd_part, gain_f):
    inner_sums = jnp.sum(grad_normed * gain_f * hidden_part, axis=1)
    return (
        rstd_part[:, None] * gain_f * grad_normed
        - hidden_part * (rstd_part**3)[:, None] * inner_sums[:, None] / D
    ).astype(jnp.bfloat16)


def local(hidden, gain, head, moment, second, labels):
    hidden_f = hidden.astype(jnp.float32)
    gain_f = gain.astype(jnp.float32)
    rstd = inverse_norm(hidden_f)
    normed = (hidden_f * rstd[:, None] * gain_f).astype(jnp.bfloat16)
    normed_all = lax.all_gather(normed, "dp", axis=0, tiled=True)
    all_labels = lax.all_gather(labels, "dp", axis=0, tiled=True)
    own_rows = head.shape[0]
    tensor_count = lax.axis_size("tensor")
    dp_count = lax.axis_size("dp")
    owner = lax.axis_index("dp") * tensor_count + lax.axis_index("tensor")
    vocab_ids = owner * own_rows + jnp.arange(own_rows, dtype=jnp.int32)
    logits = lax.dot_general(
        normed_all, head, (((1,), (1,)), ((), ())), preferred_element_type=jnp.float32
    )
    dlogits = softmax_grad(logits, all_labels, vocab_ids)
    grad_head = lax.dot_general(
        dlogits, normed_all, (((0,), (0,)), ((), ())), preferred_element_type=jnp.float32
    )
    share_rows = hidden.shape[0] // tensor_count
    ordered = dlogits.reshape(dp_count, tensor_count, share_rows, own_rows).transpose(1, 0, 2, 3)
    ordered = ordered.reshape(tensor_count * dp_count * share_rows, own_rows)
    tensor_sum = lax.psum_scatter(
        jnp.dot(ordered, head, preferred_element_type=jnp.float32).astype(jnp.bfloat16),
        "tensor",
        scatter_dimension=0,
        tiled=True,
    ).astype(jnp.float32)
    full_sum = lax.psum(tensor_sum, "dp")
    grad_normed = lax.dynamic_slice_in_dim(
        full_sum, lax.axis_index("dp") * share_rows, share_rows, 0
    )
    offset = lax.axis_index("tensor") * share_rows
    hidden_part = lax.dynamic_slice_in_dim(hidden_f, offset, share_rows, 0)
    rstd_part = lax.dynamic_slice_in_dim(rstd, offset, share_rows, 0)
    grad_gain = lax.psum(
        jnp.sum(grad_normed * hidden_part * rstd_part[:, None], axis=0), ("dp", "tensor")
    )
    part_grad = norm_backward(grad_normed, hidden_part, rstd_part, gain_f)
    grad_hidden = lax.all_gather(part_grad, "tensor", axis=0, tiled=True)
    row_sums = jnp.sum(grad_head * grad_head, axis=1)
    second_new = beta_two * second + (1.0 - beta_two) * row_sums / D
    first = beta_one * moment.astype(jnp.float32) + (1.0 - beta_one) * grad_head
    adam_step = first / bias_one / (jnp.sqrt(second_new / bias_two)[:, None] + adam_eps)
    head_new = (head.astype(jnp.float32) - step_size * adam_step).astype(jnp.bfloat16)
    return (grad_hidden, grad_gain, head_new, first.astype(jnp.bfloat16), second_new)


def wide(values):
    return values.astype(jnp.float32)


def narrow(values):
    return values.astype(jnp.bfloat16)


def fused_kernel(
    layers,
    hidden_hbm,
    gain_hbm,
    head_hbm,
    moment_hbm,
    second_ref,
    labels_ref,
    grad_hidden_ref,
    grad_gain_ref,
    head_out,
    moment_out,
    second_out,
    gathered,
    normed,
    hidden,
    gain,
    head,
    moment,
    gain_wide,
    grad_head,
    head_new,
    moment_new,
    stat_out,
    stat_near,
    stat_far,
    pair_out,
    pair_in,
    plane_out,
    plane_in,
    plane_sum,
    line_out,
    line_in,
    message,
    columns_in,
    gather_recv,
    gather_line,
    gather_plane,
    gather_pair,
    near_sems,
    far_sems,
    pair_sems,
    plane_sems,
    line_sems,
    message_send,
    message_recv,
    local_sems,
):
    groups = layers * PLANE
    tokens, width = normed.shape
    own_tokens = hidden.shape[0]
    own_rows = head.shape[0]
    half = width // 2
    quarter = half // PLANE
    piece_cols = quarter // 2
    layer_tokens = PLANE * own_tokens
    dp = lax.axis_index("dp")
    core = lax.axis_index("tensor")
    other = 1 - core
    layer = lax.div(dp, PLANE)
    spot = lax.rem(dp, PLANE)
    me = dp * 2 + core

    def across(step):
        return lax.rem(layer + step, layers)

    def beside(step):
        down = lax.rem(lax.div(spot, 2) + step // 2, 2)
        return down * 2 + lax.rem(lax.rem(spot, 2) + step % 2, 2)

    def far(step):
        return (across(step) * PLANE + spot, core)

    def near(step, flip=0):
        return (layer * PLANE + beside(step), lax.rem(core + flip, 2))

    near_steps = [(step, flip) for step in (3, 1, 2, 0) for flip in (0, 1) if step + flip]

    def remote(source, target, send_sem, recv_sem, device):
        return pltpu.make_async_remote_copy(
            src_ref=source,
            dst_ref=target,
            send_sem=send_sem,
            recv_sem=recv_sem,
            device_id=device,
            device_id_type=MESH,
        )

    loads = [
        pltpu.make_async_copy(source, target, local_sems.at[index])
        for index, (source, target) in enumerate(
            [(hidden_hbm, hidden), (gain_hbm, gain), (head_hbm, head), (moment_hbm, moment)]
        )
    ]
    for load in loads:
        load.start()

    barrier = pltpu.get_barrier_semaphore()
    for step, flip in near_steps:
        pl.semaphore_signal(barrier, inc=1, device_id=near(step, flip), device_id_type=MESH)
    for step in range(1, layers):
        pl.semaphore_signal(barrier, inc=1, device_id=far(step), device_id_type=MESH)

    loads[0].wait()
    loads[1].wait()
    gain_rows = wide(gain[...])
    for piece in range(width // LANES):
        gain_wide[:, piece * LANES : (piece + 1) * LANES] = gain_rows[piece : piece + 1]
    hidden_f = wide(hidden[...])
    rstd = lax.rsqrt(jnp.sum(hidden_f * hidden_f, axis=1, keepdims=True) / width + norm_eps)
    own = narrow(hidden_f * rstd * gain_wide[...])
    gathered[0, dp] = own[:, :half]
    gathered[1, dp] = own[:, half:]
    pl.semaphore_wait(barrier, len(near_steps) + layers - 1)

    def shard(side, group, send_sem, device):
        block = gathered.at[side, group]
        return remote(block, block, send_sem, gather_recv.at[side, group], device)

    def line_copy(step):
        return shard(core, dp, gather_line.at[step], far(step))

    def plane_copy(row, step):
        return shard(
            core,
            across(row) * PLANE + spot,
            gather_plane.at[row, step],
            near(step),
        )

    def pair_copy(side, row, step):
        group = across(row) * PLANE + beside(step)
        return shard(side, group, gather_pair.at[row, step], (dp, other))

    for step in range(1, layers):
        line_copy(step).start()
    for step in (3, 1, 2):
        plane_copy(0, step).start()
    for row in range(1, layers):
        pair_copy(core, row, 0).wait_recv()
        for step in (3, 1, 2):
            plane_copy(row, step).start()
        pair_copy(core, row, 0).start()
    for row in range(layers):
        for step in range(1, PLANE):
            pair_copy(core, row, step).wait_recv()
            pair_copy(core, row, step).start()

    def half_logits(side):
        span = pl.ds(pl.multiple_of(side * half, half), half)
        normed[:, span] = narrow(wide(gathered[side]).reshape(tokens, half))
        return lax.dot_general(
            head[:, span],
            normed[:, span],
            (((1,), (1,)), ((), ())),
            preferred_element_type=jnp.float32,
        )

    loads[2].wait()
    logits = half_logits(core)
    for row in range(layers):
        for step in range(PLANE):
            if row + step > 0:
                pair_copy(other, row, step).wait_recv()
    logits = logits + half_logits(other)

    lane = lax.broadcasted_iota(jnp.int32, (1, tokens), 1)
    targets = jnp.zeros((1, tokens), jnp.int32)
    for item in range(own_tokens):
        targets = jnp.where(lane == dp * own_tokens + item, labels_ref[item], targets)
    targets = jnp.where(core == 0, targets, 0)
    local_max = jnp.max(logits, axis=0, keepdims=True)
    local_sum = jnp.sum(jnp.exp(logits - local_max), axis=0, keepdims=True)
    place = lax.broadcasted_iota(jnp.int32, (8, tokens), 0)

    def packet(peak, total, ids):
        return jnp.where(place == 0, peak, jnp.where(place == 1, total, ids))

    def merge(packets):
        peak = packets[0][0:1]
        for item in packets[1:]:
            peak = jnp.maximum(peak, item[0:1])
        total = sum(item[1:2] * jnp.exp(item[0:1] - peak) for item in packets)
        return peak, total, sum(item[2:3] for item in packets)

    def near_move(step, flip):
        slot = step * 2 + flip
        return remote(
            stat_out.at[0],
            stat_near.at[slot],
            near_sems.at[0, slot],
            near_sems.at[1, slot],
            near(step, flip),
        )

    def far_move(step):
        return remote(
            stat_out.at[1], stat_far.at[step], far_sems.at[0, step], far_sems.at[1, step], far(step)
        )

    packets = [packet(local_max, local_sum, wide(targets))]
    stat_out[0] = packets[0]
    for step, flip in near_steps:
        near_move(step, flip).start()
    for step, flip in near_steps:
        near_move(step, flip).wait_recv()
        packets.append(stat_near[step * 2 + flip])
    packets = [packet(*merge(packets))]
    stat_out[1] = packets[0]
    for step in range(1, layers):
        far_move(step).start()
    for step in range(1, layers):
        far_move(step).wait_recv()
        packets.append(stat_far[step])
    global_max, global_sum, target_sum = merge(packets)
    all_targets = target_sum.astype(jnp.int32)
    vocab = me * own_rows + lax.broadcasted_iota(jnp.int32, (own_rows, tokens), 0)
    onehot = wide(vocab == all_targets)
    probability = jnp.exp(logits - global_max) / global_sum
    scaled = loss_scale * (probability - onehot)
    by_row = narrow(scaled)
    by_token = narrow(scaled.T)

    def partial(side, step):
        start = side * half + beside(step) * quarter
        return jnp.dot(
            by_token,
            head[:, pl.ds(pl.multiple_of(start, quarter), quarter)],
            preferred_element_type=jnp.float32,
        )

    order = [3, 1, 2, 0]

    def pair_move(step):
        return remote(
            pair_out.at[step],
            pair_in.at[step],
            pair_sems.at[0, step],
            pair_sems.at[1, step],
            (dp, other),
        )

    def plane_move(step, side):
        return remote(
            plane_out.at[step, side],
            plane_in.at[step, side],
            plane_sems.at[0, step, side],
            plane_sems.at[1, step, side],
            near(step),
        )

    def line_move(step, side):
        return remote(
            line_out.at[step, side],
            line_in.at[step, side],
            line_sems.at[0, step, side],
            line_sems.at[1, step, side],
            far(step),
        )

    for step in order:
        pair_out[step] = narrow(partial(other, step))
        pair_move(step).start()
    for step in order:
        mine = partial(core, step)
        pair_move(step).wait_recv()
        mine = mine + wide(pair_in[step])
        for side in range(2):
            part = mine[:, side * piece_cols : (side + 1) * piece_cols]
            if step > 0:
                plane_out[step, side] = narrow(part)
                plane_move(step, side).start()
            else:
                plane_sum[side] = part

    squares = jnp.zeros((own_rows, 1), jnp.float32)
    for start in range(0, width, CHUNK):
        piece = jnp.dot(
            by_row, normed[:, start : start + CHUNK], preferred_element_type=jnp.float32
        )
        grad_head[:, start : start + CHUNK] = piece
        squares = squares + jnp.sum(piece * piece, axis=1, keepdims=True)
    second_wide = jnp.broadcast_to(second_ref[...], (LANES, own_rows)).T
    second_new = beta_two * second_wide + (1.0 - beta_two) * squares / width
    second_out[...] = second_new.T[0:1, :]
    scale = (step_size / bias_one) / (jnp.sqrt(second_new / bias_two) + adam_eps)
    scale = scale[:, 0:1]
    loads[3].wait()

    def adam(index, carry):
        span = pl.ds(pl.multiple_of(index * CHUNK, CHUNK), CHUNK)
        first = beta_one * wide(moment[:, span]) + (1.0 - beta_one) * grad_head[:, span]
        moment_new[:, span] = narrow(first)
        head_new[:, span] = narrow(wide(head[:, span]) - first * scale)
        return carry

    lax.fori_loop(0, width // CHUNK, adam, 0)
    stores = [
        pltpu.make_async_copy(head_new, head_out, local_sems.at[4]),
        pltpu.make_async_copy(moment_new, moment_out, local_sems.at[5]),
    ]
    for store in stores:
        store.start()

    def tail_rows(values, rows):
        high = wide(narrow(values))
        row = lax.broadcasted_iota(jnp.int32, (rows, values.shape[1]), 0)
        return jnp.where(row == 0, high, jnp.where(row == 1, values - high, 0.0))

    def layer_rows(step):
        start = across(step) * layer_tokens
        return pl.ds(pl.multiple_of(start, layer_tokens), layer_tokens)

    gain_parts = []
    for side in range(2):
        total = plane_sum[side]
        for step in (3, 1, 2):
            plane_move(step, side).wait_recv()
            total = total + wide(plane_in[step, side])
        plane_sum[side] = total
        for step in range(1, layers):
            line_out[step, side, :layer_tokens] = narrow(plane_sum[side, layer_rows(step), :])
        start = core * half + spot * quarter + side * piece_cols
        span = pl.ds(pl.multiple_of(start, piece_cols), piece_cols)
        gain_part = jnp.sum(total * wide(normed[:, span]), axis=0, keepdims=True)
        gain_part = gain_part / gain_wide[:, span]
        gain_parts.append(gain_part)
        tail = narrow(tail_rows(gain_part, 16))
        for step in range(1, layers):
            line_out[step, side, layer_tokens:] = tail
            line_move(step, side).start()

    sums, gains = [], []
    for side in range(2):
        part = plane_sum[side, layer_rows(0), :]
        gain_part = gain_parts[side]
        for step in range(1, layers):
            line_move(step, side).wait_recv()
            arrived = wide(line_in[step, side])
            part = part + arrived[:layer_tokens]
            gain_part = (
                gain_part
                + arrived[layer_tokens : layer_tokens + 1]
                + arrived[layer_tokens + 1 : layer_tokens + 2]
            )
        sums.append(part)
        gains.append(gain_part)
    sums = jnp.concatenate(sums, axis=1).reshape(PLANE, own_tokens, quarter)
    tail = tail_rows(jnp.concatenate(gains, axis=1), own_tokens)
    tail = jnp.broadcast_to(tail[None], sums.shape)
    message[...] = narrow(jnp.concatenate([sums, tail], axis=1))
    own_block = core * PLANE + spot

    def message_move(step, flip, block):
        slot = step * 2 + flip
        return remote(
            message.at[beside(step)],
            columns_in.at[block],
            message_send.at[slot],
            message_recv.at[block],
            near(step, flip),
        )

    for step, flip in near_steps:
        message_move(step, flip, own_block).start()
    columns_in[own_block] = message[spot]

    for step in range(1, layers):
        line_copy(step).wait_send()
        far_move(step).wait_send()
        for side in range(2):
            line_move(step, side).wait_send()
    for row in range(layers):
        for step in range(PLANE):
            if step > 0:
                plane_copy(row, step).wait_send()
            if row + step > 0:
                pair_copy(core, row, step).wait_send()
    for step in range(PLANE):
        pair_move(step).wait_send()
        if step > 0:
            for side in range(2):
                plane_move(step, side).wait_send()
    for step, flip in near_steps:
        near_move(step, flip).wait_send()
    for step, flip in near_steps:
        source = lax.rem(core + flip, 2) * PLANE + beside(step)
        message_move(step, flip, source).wait_recv()

    pieces = []
    lines = quarter // LANES
    for block in range(2 * PLANE):
        arrived = wide(columns_in[block])
        pieces.append(arrived[:own_tokens])
        gain_row = (
            arrived[own_tokens : own_tokens + 1] + arrived[own_tokens + 1 : own_tokens + 2]
        )
        for line in range(lines):
            place = block * lines + line
            grad_gain_ref[place : place + 1, :] = gain_row[:, line * LANES : (line + 1) * LANES]
    summed = jnp.concatenate(pieces, axis=1) * gain_wide[...]
    inner = jnp.sum(summed * hidden_f, axis=1, keepdims=True)
    grad_hidden_ref[...] = narrow(
        rstd * summed - hidden_f * (rstd * rstd * rstd * inner / width)
    )
    for step, flip in near_steps:
        message_move(step, flip, own_block).wait_send()
    for store in stores:
        store.wait()


def fused(groups, hidden, gain, head, moment, second, labels):
    own_tokens, width = hidden.shape
    own_rows = head.shape[0]
    layers = groups // PLANE
    tokens = groups * own_tokens
    devices = groups * 2
    bf16, f32 = jnp.bfloat16, jnp.float32
    quarter = width // 2 // PLANE
    vmem = pl.BlockSpec(memory_space=pltpu.VMEM)
    hbm = pl.BlockSpec(memory_space=pltpu.HBM)
    dma = pltpu.SemaphoreType.DMA
    grad_hidden, grad_gain, head_new, moment_new, second_new = pl.pallas_call(
        functools.partial(fused_kernel, layers),
        out_shape=(
            jax.ShapeDtypeStruct(hidden.shape, bf16),
            jax.ShapeDtypeStruct((devices, LANES), f32),
            jax.ShapeDtypeStruct(head.shape, bf16),
            jax.ShapeDtypeStruct(head.shape, bf16),
            jax.ShapeDtypeStruct((1, own_rows), f32),
        ),
        in_specs=[hbm, hbm, hbm, hbm, vmem, pl.BlockSpec(memory_space=pltpu.SMEM)],
        out_specs=(vmem, vmem, hbm, hbm, vmem),
        scratch_shapes=[
            pltpu.VMEM((2, groups, own_tokens, width // 2), bf16),
            pltpu.VMEM((tokens, width), bf16),
            pltpu.VMEM(hidden.shape, bf16),
            pltpu.VMEM((width // LANES, LANES), bf16),
            pltpu.VMEM((own_rows, width), bf16),
            pltpu.VMEM((own_rows, width), bf16),
            pltpu.VMEM((1, width), f32),
            pltpu.VMEM((own_rows, width), f32),
            pltpu.VMEM((own_rows, width), bf16),
            pltpu.VMEM((own_rows, width), bf16),
            pltpu.VMEM((2, 8, tokens), f32),
            pltpu.VMEM((2 * PLANE, 8, tokens), f32),
            pltpu.VMEM((layers, 8, tokens), f32),
            pltpu.VMEM((PLANE, tokens, quarter), bf16),
            pltpu.VMEM((PLANE, tokens, quarter), bf16),
            pltpu.VMEM((PLANE, 2, tokens, quarter // 2), bf16),
            pltpu.VMEM((PLANE, 2, tokens, quarter // 2), bf16),
            pltpu.VMEM((2, tokens, quarter // 2), f32),
            pltpu.VMEM((layers, 2, PLANE * own_tokens + 16, quarter // 2), bf16),
            pltpu.VMEM((layers, 2, PLANE * own_tokens + 16, quarter // 2), bf16),
            pltpu.VMEM((PLANE, 2 * own_tokens, quarter), bf16),
            pltpu.VMEM((2 * PLANE, 2 * own_tokens, quarter), bf16),
            dma((2, groups)),
            dma((layers,)),
            dma((layers, PLANE)),
            dma((layers, PLANE)),
            dma((2, 2 * PLANE)),
            dma((2, layers)),
            dma((2, PLANE)),
            dma((2, PLANE, 2)),
            dma((2, layers, 2)),
            dma((2 * PLANE,)),
            dma((2 * PLANE,)),
            dma((6,)),
        ],
        compiler_params=pltpu.CompilerParams(
            collective_id=0, has_side_effects=True, vmem_limit_bytes=VMEM_BYTES
        ),
    )(hidden, gain.reshape(width // LANES, LANES), head, moment, second.reshape(1, own_rows), labels)
    return settle(grad_hidden, grad_gain, head_new, moment_new, second_new)


def settle_kernel(count, *refs):
    held, sems = refs[2 * count : -1], refs[-1]
    loads = [
        pltpu.make_async_copy(refs[i], held[i], sems.at[0, i]) for i in range(count)
    ]
    stores = [
        pltpu.make_async_copy(held[i], refs[count + i], sems.at[1, i]) for i in range(count)
    ]
    for load in loads:
        load.start()
    for load, store in zip(loads, stores):
        load.wait()
        store.start()
    for store in stores:
        store.wait()


def settle(*results):
    hbm = pl.BlockSpec(memory_space=pltpu.HBM)
    count = len(results)
    settled = pl.pallas_call(
        functools.partial(settle_kernel, count),
        out_shape=tuple(jax.ShapeDtypeStruct(x.shape, x.dtype) for x in results),
        in_specs=[hbm] * count,
        out_specs=(hbm,) * count,
        scratch_shapes=[pltpu.VMEM(x.shape, x.dtype) for x in results]
        + [pltpu.SemaphoreType.DMA((2, count))],
        compiler_params=pltpu.CompilerParams(vmem_limit_bytes=VMEM_BYTES),
    )(*results)
    grad_hidden, grad_gain, head_new, moment_new, second_new = settled
    return grad_hidden, grad_gain.reshape(-1), head_new, moment_new, second_new.reshape(-1)


def fits(mesh, hidden, head):
    groups, cores = mesh.shape["dp"], mesh.shape["tensor"]
    return (
        cores == 2
        and groups % PLANE == 0
        and hidden.shape[0] == LANES
        and hidden.shape[1] % (groups * cores * LANES) == 0
        and hidden.shape[0] == groups * 8
        and head.shape[0] == groups * cores * LANES
    )


def solution(mesh):
    placed = (
        P("dp", None),
        P(),
        P(("dp", "tensor"), None),
        P(("dp", "tensor"), None),
        P(("dp", "tensor")),
        P("dp"),
    )

    def whole(hidden, gain, head, moment, second, labels):
        body = local
        if fits(mesh, hidden, head):
            body = functools.partial(fused, mesh.shape["dp"])
        return jax.shard_map(
            body,
            mesh=mesh,
            in_specs=placed,
            out_specs=(
                P("dp", None),
                P(),
                P(("dp", "tensor"), None),
                P(("dp", "tensor"), None),
                P(("dp", "tensor")),
            ),
            check_vma=False,
        )(hidden, gain, head, moment, second, labels)

    return whole
```

```python
import functools

import jax
import jax.numpy as jnp
from jax import lax
from jax.experimental import pallas as pl
from jax.experimental.pallas import tpu as pltpu
from jax.sharding import PartitionSpec as P

MESH = pl.DeviceIdType.MESH
LANES = 128
PLANE = 4
CHUNK = 512
VMEM_BYTES = 61440 * 1024
SETTLE_PARTS = 4

D = 4096


loss_scale = 16.0
beta_one = 0.9
beta_two = 0.999
adam_eps = 1e-08
step_size = 0.02
norm_eps = 1e-05
bias_one = 1.0 - 0.9**10
bias_two = 1.0 - 0.999**10


def inverse_norm(values_f):
    squares = jnp.sum(values_f * values_f, axis=1)
    return lax.rsqrt(squares / D + norm_eps)


def softmax_grad(logits, targets, vocab_ids):
    local_max = jnp.max(logits, axis=1)
    local_sum = jnp.sum(jnp.exp(logits - local_max[:, None]), axis=1)
    global_max = lax.pmax(local_max, ("dp", "tensor"))
    global_sum = lax.psum(local_sum * jnp.exp(local_max - global_max), ("dp", "tensor"))
    onehot = (targets[:, None] == vocab_ids[None, :]).astype(jnp.float32)
    probability = jnp.exp(logits - global_max[:, None]) / global_sum[:, None]
    return (loss_scale * (probability - onehot)).astype(jnp.bfloat16)


def norm_backward(grad_normed, hidden_part, rstd_part, gain_f):
    inner_sums = jnp.sum(grad_normed * gain_f * hidden_part, axis=1)
    return (
        rstd_part[:, None] * gain_f * grad_normed
        - hidden_part * (rstd_part**3)[:, None] * inner_sums[:, None] / D
    ).astype(jnp.bfloat16)


def local(hidden, gain, head, moment, second, labels):
    hidden_f = hidden.astype(jnp.float32)
    gain_f = gain.astype(jnp.float32)
    rstd = inverse_norm(hidden_f)
    normed = (hidden_f * rstd[:, None] * gain_f).astype(jnp.bfloat16)
    normed_all = lax.all_gather(normed, "dp", axis=0, tiled=True)
    all_labels = lax.all_gather(labels, "dp", axis=0, tiled=True)
    own_rows = head.shape[0]
    tensor_count = lax.axis_size("tensor")
    dp_count = lax.axis_size("dp")
    owner = lax.axis_index("dp") * tensor_count + lax.axis_index("tensor")
    vocab_ids = owner * own_rows + jnp.arange(own_rows, dtype=jnp.int32)
    logits = lax.dot_general(
        normed_all, head, (((1,), (1,)), ((), ())), preferred_element_type=jnp.float32
    )
    dlogits = softmax_grad(logits, all_labels, vocab_ids)
    grad_head = lax.dot_general(
        dlogits, normed_all, (((0,), (0,)), ((), ())), preferred_element_type=jnp.float32
    )
    share_rows = hidden.shape[0] // tensor_count
    ordered = dlogits.reshape(dp_count, tensor_count, share_rows, own_rows).transpose(1, 0, 2, 3)
    ordered = ordered.reshape(tensor_count * dp_count * share_rows, own_rows)
    tensor_sum = lax.psum_scatter(
        jnp.dot(ordered, head, preferred_element_type=jnp.float32).astype(jnp.bfloat16),
        "tensor",
        scatter_dimension=0,
        tiled=True,
    ).astype(jnp.float32)
    full_sum = lax.psum(tensor_sum, "dp")
    grad_normed = lax.dynamic_slice_in_dim(
        full_sum, lax.axis_index("dp") * share_rows, share_rows, 0
    )
    offset = lax.axis_index("tensor") * share_rows
    hidden_part = lax.dynamic_slice_in_dim(hidden_f, offset, share_rows, 0)
    rstd_part = lax.dynamic_slice_in_dim(rstd, offset, share_rows, 0)
    grad_gain = lax.psum(
        jnp.sum(grad_normed * hidden_part * rstd_part[:, None], axis=0), ("dp", "tensor")
    )
    part_grad = norm_backward(grad_normed, hidden_part, rstd_part, gain_f)
    grad_hidden = lax.all_gather(part_grad, "tensor", axis=0, tiled=True)
    row_sums = jnp.sum(grad_head * grad_head, axis=1)
    second_new = beta_two * second + (1.0 - beta_two) * row_sums / D
    first = beta_one * moment.astype(jnp.float32) + (1.0 - beta_one) * grad_head
    adam_step = first / bias_one / (jnp.sqrt(second_new / bias_two)[:, None] + adam_eps)
    head_new = (head.astype(jnp.float32) - step_size * adam_step).astype(jnp.bfloat16)
    return (grad_hidden, grad_gain, head_new, first.astype(jnp.bfloat16), second_new)


def wide(values):
    return values.astype(jnp.float32)


def narrow(values):
    return values.astype(jnp.bfloat16)


def fused_kernel(
    layers,
    hidden_hbm,
    gain_hbm,
    head_hbm,
    moment_hbm,
    second_ref,
    labels_ref,
    grad_hidden_ref,
    grad_gain_ref,
    head_out,
    moment_out,
    second_out,
    gathered,
    normed,
    hidden,
    gain,
    head,
    moment,
    gain_wide,
    grad_head,
    head_new,
    moment_new,
    stat_out,
    stat_near,
    stat_far,
    pair_out,
    pair_in,
    plane_out,
    plane_in,
    plane_sum,
    line_out,
    line_in,
    message,
    columns_in,
    gather_recv,
    gather_line,
    gather_plane,
    gather_pair,
    near_sems,
    far_sems,
    pair_sems,
    plane_sems,
    line_sems,
    message_send,
    message_recv,
    local_sems,
):
    groups = layers * PLANE
    tokens, width = normed.shape
    own_tokens = hidden.shape[0]
    own_rows = head.shape[0]
    half = width // 2
    quarter = half // PLANE
    piece_cols = quarter // 2
    layer_tokens = PLANE * own_tokens
    dp = lax.axis_index("dp")
    core = lax.axis_index("tensor")
    other = 1 - core
    layer = lax.div(dp, PLANE)
    spot = lax.rem(dp, PLANE)
    me = dp * 2 + core

    def across(step):
        return lax.rem(layer + step, layers)

    def beside(step):
        down = lax.rem(lax.div(spot, 2) + step // 2, 2)
        return down * 2 + lax.rem(lax.rem(spot, 2) + step % 2, 2)

    def far(step):
        return (across(step) * PLANE + spot, core)

    def near(step, flip=0):
        return (layer * PLANE + beside(step), lax.rem(core + flip, 2))

    near_steps = [(step, flip) for step in (3, 1, 2, 0) for flip in (0, 1) if step + flip]

    def remote(source, target, send_sem, recv_sem, device):
        return pltpu.make_async_remote_copy(
            src_ref=source,
            dst_ref=target,
            send_sem=send_sem,
            recv_sem=recv_sem,
            device_id=device,
            device_id_type=MESH,
        )

    loads = [
        pltpu.make_async_copy(source, target, local_sems.at[index])
        for index, (source, target) in enumerate(
            [(hidden_hbm, hidden), (gain_hbm, gain), (head_hbm, head), (moment_hbm, moment)]
        )
    ]
    for load in loads:
        load.start()

    barrier = pltpu.get_barrier_semaphore()
    for step, flip in near_steps:
        pl.semaphore_signal(barrier, inc=1, device_id=near(step, flip), device_id_type=MESH)
    for step in range(1, layers):
        pl.semaphore_signal(barrier, inc=1, device_id=far(step), device_id_type=MESH)

    loads[0].wait()
    loads[1].wait()
    gain_rows = wide(gain[...])
    for piece in range(width // LANES):
        gain_wide[:, piece * LANES : (piece + 1) * LANES] = gain_rows[piece : piece + 1]
    hidden_f = wide(hidden[...])
    rstd = lax.rsqrt(jnp.sum(hidden_f * hidden_f, axis=1, keepdims=True) / width + norm_eps)
    own = narrow(hidden_f * rstd * gain_wide[...])
    gathered[0, dp] = own[:, :half]
    gathered[1, dp] = own[:, half:]
    pl.semaphore_wait(barrier, len(near_steps) + layers - 1)

    def shard(side, group, send_sem, device):
        block = gathered.at[side, group]
        return remote(block, block, send_sem, gather_recv.at[side, group], device)

    def line_copy(step):
        return shard(core, dp, gather_line.at[step], far(step))

    def plane_copy(row, step):
        return shard(
            core,
            across(row) * PLANE + spot,
            gather_plane.at[row, step],
            near(step),
        )

    def pair_copy(side, row, step):
        group = across(row) * PLANE + beside(step)
        return shard(side, group, gather_pair.at[row, step], (dp, other))

    def columns_of(side):
        return pl.ds(pl.multiple_of(side * half, half), half)

    def take(side, row):
        first = across(row)
        blocks = wide(gathered[side, pl.ds(first * PLANE, PLANE)])
        span = pl.ds(pl.multiple_of(first * layer_tokens, layer_tokens), layer_tokens)
        normed[span, columns_of(side)] = narrow(blocks.reshape(layer_tokens, half))

    for step in range(1, layers):
        line_copy(step).start()
    for step in (3, 1, 2):
        plane_copy(0, step).start()
    for row in range(1, layers):
        pair_copy(core, row, 0).wait_recv()
        for step in (3, 1, 2):
            plane_copy(row, step).start()
        pair_copy(core, row, 0).start()
    for row in range(layers):
        for step in range(1, PLANE):
            pair_copy(core, row, step).wait_recv()
            pair_copy(core, row, step).start()
        take(core, row)

    def half_logits(side):
        span = columns_of(side)
        return lax.dot_general(
            head[:, span],
            normed[:, span],
            (((1,), (1,)), ((), ())),
            preferred_element_type=jnp.float32,
        )

    loads[2].wait()
    logits = half_logits(core)
    for row in range(layers):
        for step in range(PLANE):
            if row + step > 0:
                pair_copy(other, row, step).wait_recv()
        take(other, row)
    logits = logits + half_logits(other)

    lane = lax.broadcasted_iota(jnp.int32, (1, tokens), 1)
    targets = jnp.zeros((1, tokens), jnp.int32)
    for item in range(own_tokens):
        targets = jnp.where(lane == dp * own_tokens + item, labels_ref[item], targets)
    targets = jnp.where(core == 0, targets, 0)
    local_max = jnp.max(logits, axis=0, keepdims=True)
    local_sum = jnp.sum(jnp.exp(logits - local_max), axis=0, keepdims=True)
    place = lax.broadcasted_iota(jnp.int32, (8, tokens), 0)

    def packet(peak, total, ids):
        return jnp.where(place == 0, peak, jnp.where(place == 1, total, ids))

    def merge(packets):
        peak = packets[0][0:1]
        for item in packets[1:]:
            peak = jnp.maximum(peak, item[0:1])
        total = sum(item[1:2] * jnp.exp(item[0:1] - peak) for item in packets)
        return peak, total, sum(item[2:3] for item in packets)

    def near_move(step, flip):
        slot = step * 2 + flip
        return remote(
            stat_out.at[0],
            stat_near.at[slot],
            near_sems.at[0, slot],
            near_sems.at[1, slot],
            near(step, flip),
        )

    def far_move(step):
        return remote(
            stat_out.at[1], stat_far.at[step], far_sems.at[0, step], far_sems.at[1, step], far(step)
        )

    packets = [packet(local_max, local_sum, wide(targets))]
    stat_out[0] = packets[0]
    for step, flip in near_steps:
        near_move(step, flip).start()
    for step, flip in near_steps:
        near_move(step, flip).wait_recv()
        packets.append(stat_near[step * 2 + flip])
    packets = [packet(*merge(packets))]
    stat_out[1] = packets[0]
    for step in range(1, layers):
        far_move(step).start()
    for step in range(1, layers):
        far_move(step).wait_recv()
        packets.append(stat_far[step])
    global_max, global_sum, target_sum = merge(packets)
    all_targets = target_sum.astype(jnp.int32)
    vocab = me * own_rows + lax.broadcasted_iota(jnp.int32, (own_rows, tokens), 0)
    onehot = wide(vocab == all_targets)
    probability = jnp.exp(logits - global_max) / global_sum
    scaled = loss_scale * (probability - onehot)
    by_row = narrow(scaled)
    by_token = narrow(scaled.T)

    def partial(side, step):
        start = side * half + beside(step) * quarter
        return jnp.dot(
            by_token,
            head[:, pl.ds(pl.multiple_of(start, quarter), quarter)],
            preferred_element_type=jnp.float32,
        )

    order = [3, 1, 2, 0]

    def pair_move(step):
        return remote(
            pair_out.at[step],
            pair_in.at[step],
            pair_sems.at[0, step],
            pair_sems.at[1, step],
            (dp, other),
        )

    def plane_move(step, side):
        return remote(
            plane_out.at[step, side],
            plane_in.at[step, side],
            plane_sems.at[0, step, side],
            plane_sems.at[1, step, side],
            near(step),
        )

    def line_move(step, side):
        return remote(
            line_out.at[step, side],
            line_in.at[step, side],
            line_sems.at[0, step, side],
            line_sems.at[1, step, side],
            far(step),
        )

    for step in order:
        pair_out[step] = narrow(partial(other, step))
        pair_move(step).start()
    for step in order:
        mine = partial(core, step)
        pair_move(step).wait_recv()
        mine = mine + wide(pair_in[step])
        for side in range(2):
            part = mine[:, side * piece_cols : (side + 1) * piece_cols]
            if step > 0:
                plane_out[step, side] = narrow(part)
                plane_move(step, side).start()
            else:
                plane_sum[side] = part

    squares = jnp.zeros((own_rows, 1), jnp.float32)
    for start in range(0, width, CHUNK):
        piece = jnp.dot(
            by_row, normed[:, start : start + CHUNK], preferred_element_type=jnp.float32
        )
        grad_head[:, start : start + CHUNK] = piece
        squares = squares + jnp.sum(piece * piece, axis=1, keepdims=True)
    second_wide = jnp.broadcast_to(second_ref[...], (LANES, own_rows)).T
    second_new = beta_two * second_wide + (1.0 - beta_two) * squares / width
    second_out[...] = second_new.T[0:1, :]
    scale = (step_size / bias_one) / (jnp.sqrt(second_new / bias_two) + adam_eps)
    scale = scale[:, 0:1]
    loads[3].wait()

    def adam(index, carry):
        span = pl.ds(pl.multiple_of(index * CHUNK, CHUNK), CHUNK)
        first = beta_one * wide(moment[:, span]) + (1.0 - beta_one) * grad_head[:, span]
        moment_new[:, span] = narrow(first)
        head_new[:, span] = narrow(wide(head[:, span]) - first * scale)
        return carry

    lax.fori_loop(0, width // CHUNK, adam, 0)
    stores = [
        pltpu.make_async_copy(head_new, head_out, local_sems.at[4]),
        pltpu.make_async_copy(moment_new, moment_out, local_sems.at[5]),
    ]
    for store in stores:
        store.start()

    def tail_rows(values, rows):
        high = wide(narrow(values))
        row = lax.broadcasted_iota(jnp.int32, (rows, values.shape[1]), 0)
        return jnp.where(row == 0, high, jnp.where(row == 1, values - high, 0.0))

    def layer_rows(step):
        start = across(step) * layer_tokens
        return pl.ds(pl.multiple_of(start, layer_tokens), layer_tokens)

    gain_parts = []
    for side in range(2):
        total = plane_sum[side]
        for step in (3, 1, 2):
            plane_move(step, side).wait_recv()
            total = total + wide(plane_in[step, side])
        plane_sum[side] = total
        for step in range(1, layers):
            line_out[step, side, :layer_tokens] = narrow(plane_sum[side, layer_rows(step), :])
        start = core * half + spot * quarter + side * piece_cols
        span = pl.ds(pl.multiple_of(start, piece_cols), piece_cols)
        gain_part = jnp.sum(total * wide(normed[:, span]), axis=0, keepdims=True)
        gain_part = gain_part / gain_wide[:, span]
        gain_parts.append(gain_part)
        tail = narrow(tail_rows(gain_part, 16))
        for step in range(1, layers):
            line_out[step, side, layer_tokens:] = tail
            line_move(step, side).start()

    sums, gains = [], []
    for side in range(2):
        part = plane_sum[side, layer_rows(0), :]
        gain_part = gain_parts[side]
        for step in range(1, layers):
            line_move(step, side).wait_recv()
            arrived = wide(line_in[step, side])
            part = part + arrived[:layer_tokens]
            gain_part = (
                gain_part
                + arrived[layer_tokens : layer_tokens + 1]
                + arrived[layer_tokens + 1 : layer_tokens + 2]
            )
        sums.append(part)
        gains.append(gain_part)
    sums = jnp.concatenate(sums, axis=1).reshape(PLANE, own_tokens, quarter)
    tail = tail_rows(jnp.concatenate(gains, axis=1), own_tokens)
    tail = jnp.broadcast_to(tail[None], sums.shape)
    message[...] = narrow(jnp.concatenate([sums, tail], axis=1))
    own_block = core * PLANE + spot

    def message_move(step, flip, block):
        slot = step * 2 + flip
        return remote(
            message.at[beside(step)],
            columns_in.at[block],
            message_send.at[slot],
            message_recv.at[block],
            near(step, flip),
        )

    for step, flip in near_steps:
        message_move(step, flip, own_block).start()
    columns_in[own_block] = message[spot]

    for step in range(1, layers):
        line_copy(step).wait_send()
        far_move(step).wait_send()
        for side in range(2):
            line_move(step, side).wait_send()
    for row in range(layers):
        for step in range(PLANE):
            if step > 0:
                plane_copy(row, step).wait_send()
            if row + step > 0:
                pair_copy(core, row, step).wait_send()
    for step in range(PLANE):
        pair_move(step).wait_send()
        if step > 0:
            for side in range(2):
                plane_move(step, side).wait_send()
    for step, flip in near_steps:
        near_move(step, flip).wait_send()
    for step, flip in near_steps:
        source = lax.rem(core + flip, 2) * PLANE + beside(step)
        message_move(step, flip, source).wait_recv()

    pieces = []
    lines = quarter // LANES
    for block in range(2 * PLANE):
        arrived = wide(columns_in[block])
        pieces.append(arrived[:own_tokens])
        gain_row = (
            arrived[own_tokens : own_tokens + 1] + arrived[own_tokens + 1 : own_tokens + 2]
        )
        for line in range(lines):
            place = block * lines + line
            grad_gain_ref[place : place + 1, :] = gain_row[:, line * LANES : (line + 1) * LANES]
    summed = jnp.concatenate(pieces, axis=1) * gain_wide[...]
    inner = jnp.sum(summed * hidden_f, axis=1, keepdims=True)
    grad_hidden_ref[...] = narrow(
        rstd * summed - hidden_f * (rstd * rstd * rstd * inner / width)
    )
    for step, flip in near_steps:
        message_move(step, flip, own_block).wait_send()
    for store in stores:
        store.wait()


def fused(groups, hidden, gain, head, moment, second, labels):
    own_tokens, width = hidden.shape
    own_rows = head.shape[0]
    layers = groups // PLANE
    tokens = groups * own_tokens
    devices = groups * 2
    bf16, f32 = jnp.bfloat16, jnp.float32
    quarter = width // 2 // PLANE
    vmem = pl.BlockSpec(memory_space=pltpu.VMEM)
    hbm = pl.BlockSpec(memory_space=pltpu.HBM)
    dma = pltpu.SemaphoreType.DMA
    grad_hidden, grad_gain, head_new, moment_new, second_new = pl.pallas_call(
        functools.partial(fused_kernel, layers),
        out_shape=(
            jax.ShapeDtypeStruct(hidden.shape, bf16),
            jax.ShapeDtypeStruct((devices, LANES), f32),
            jax.ShapeDtypeStruct(head.shape, bf16),
            jax.ShapeDtypeStruct(head.shape, bf16),
            jax.ShapeDtypeStruct((1, own_rows), f32),
        ),
        in_specs=[hbm, hbm, hbm, hbm, vmem, pl.BlockSpec(memory_space=pltpu.SMEM)],
        out_specs=(vmem, vmem, hbm, hbm, vmem),
        scratch_shapes=[
            pltpu.VMEM((2, groups, own_tokens, width // 2), bf16),
            pltpu.VMEM((tokens, width), bf16),
            pltpu.VMEM(hidden.shape, bf16),
            pltpu.VMEM((width // LANES, LANES), bf16),
            pltpu.VMEM((own_rows, width), bf16),
            pltpu.VMEM((own_rows, width), bf16),
            pltpu.VMEM((1, width), f32),
            pltpu.VMEM((own_rows, width), f32),
            pltpu.VMEM((own_rows, width), bf16),
            pltpu.VMEM((own_rows, width), bf16),
            pltpu.VMEM((2, 8, tokens), f32),
            pltpu.VMEM((2 * PLANE, 8, tokens), f32),
            pltpu.VMEM((layers, 8, tokens), f32),
            pltpu.VMEM((PLANE, tokens, quarter), bf16),
            pltpu.VMEM((PLANE, tokens, quarter), bf16),
            pltpu.VMEM((PLANE, 2, tokens, quarter // 2), bf16),
            pltpu.VMEM((PLANE, 2, tokens, quarter // 2), bf16),
            pltpu.VMEM((2, tokens, quarter // 2), f32),
            pltpu.VMEM((layers, 2, PLANE * own_tokens + 16, quarter // 2), bf16),
            pltpu.VMEM((layers, 2, PLANE * own_tokens + 16, quarter // 2), bf16),
            pltpu.VMEM((PLANE, 2 * own_tokens, quarter), bf16),
            pltpu.VMEM((2 * PLANE, 2 * own_tokens, quarter), bf16),
            dma((2, groups)),
            dma((layers,)),
            dma((layers, PLANE)),
            dma((layers, PLANE)),
            dma((2, 2 * PLANE)),
            dma((2, layers)),
            dma((2, PLANE)),
            dma((2, PLANE, 2)),
            dma((2, layers, 2)),
            dma((2 * PLANE,)),
            dma((2 * PLANE,)),
            dma((6,)),
        ],
        compiler_params=pltpu.CompilerParams(
            collective_id=0, has_side_effects=True, vmem_limit_bytes=VMEM_BYTES
        ),
    )(hidden, gain.reshape(width // LANES, LANES), head, moment, second.reshape(1, own_rows), labels)
    return settle(grad_hidden, grad_gain, head_new, moment_new, second_new)


def settle_kernel(count, *refs):
    held, sems = refs[2 * count : -1], refs[-1]
    loads, stores = [], []
    for index in range(count):
        rows = held[index].shape[0]
        parts = SETTLE_PARTS if rows % (SETTLE_PARTS * 16) == 0 else 1
        for part in range(parts):
            span = pl.ds(part * (rows // parts), rows // parts)
            slot = index * SETTLE_PARTS + part
            source, middle, target = (
                ref.at[span] for ref in (refs[index], held[index], refs[count + index])
            )
            loads.append(pltpu.make_async_copy(source, middle, sems.at[0, slot]))
            stores.append(pltpu.make_async_copy(middle, target, sems.at[1, slot]))
    for load in loads:
        load.start()
    for load, store in zip(loads, stores):
        load.wait()
        store.start()
    for store in stores:
        store.wait()


def settle(*results):
    hbm = pl.BlockSpec(memory_space=pltpu.HBM)
    count = len(results)
    settled = pl.pallas_call(
        functools.partial(settle_kernel, count),
        out_shape=tuple(jax.ShapeDtypeStruct(x.shape, x.dtype) for x in results),
        in_specs=[hbm] * count,
        out_specs=(hbm,) * count,
        scratch_shapes=[pltpu.VMEM(x.shape, x.dtype) for x in results]
        + [pltpu.SemaphoreType.DMA((2, count * SETTLE_PARTS))],
        compiler_params=pltpu.CompilerParams(vmem_limit_bytes=VMEM_BYTES),
    )(*results)
    grad_hidden, grad_gain, head_new, moment_new, second_new = settled
    return grad_hidden, grad_gain.reshape(-1), head_new, moment_new, second_new.reshape(-1)


def fits(mesh, hidden, head):
    groups, cores = mesh.shape["dp"], mesh.shape["tensor"]
    return (
        cores == 2
        and groups % PLANE == 0
        and hidden.shape[0] == LANES
        and hidden.shape[1] % (groups * cores * LANES) == 0
        and hidden.shape[0] == groups * 8
        and head.shape[0] == groups * cores * LANES
    )


def solution(mesh):
    placed = (
        P("dp", None),
        P(),
        P(("dp", "tensor"), None),
        P(("dp", "tensor"), None),
        P(("dp", "tensor")),
        P("dp"),
    )

    def whole(hidden, gain, head, moment, second, labels):
        body = local
        if fits(mesh, hidden, head):
            body = functools.partial(fused, mesh.shape["dp"])
        return jax.shard_map(
            body,
            mesh=mesh,
            in_specs=placed,
            out_specs=(
                P("dp", None),
                P(),
                P(("dp", "tensor"), None),
                P(("dp", "tensor"), None),
                P(("dp", "tensor")),
            ),
            check_vma=False,
        )(hidden, gain, head, moment, second, labels)

    return whole
```
